1024 devices in a mesh: row: 16 (over y, x), col: 64 (over z, core).
Axes of the slice: x: 4, y: 4, z: 32, core: 2. Of those that a mesh axis runs over, the one named last changes fastest.
Arguments:
- evecs: float32 [8192, 8192], P('row', 'col'), may hold values from -6 to 6
- offsets: int32 [4, 2], replicated, may hold values from 0 to 127, as said below
- refl: float32 [4, 2, 64, 64, 192], P(None, None, 'row', 'col'), may hold values from -6 to 6, as said below
Outputs:
- rotated: float32 [8192, 8192], P('row', 'col')
The draws below stay inside these ranges and needn't reach their ends.
Inputs may be any that keep to these rules, and one draw needn't show every extreme that they name: Within each round and sweep the windows start at offsets plus multiples of 128; some entry is 0 and some is 127 in every draw. `refl`: each block's triangular factor T is the inverse of the strictly upper part of V^T V plus half its diagonal, so that I - V T V^T is orthogonal.
All inputs are finite; a program needn't handle non-finite values.
Results may differ from the reference program's by a relative error of at most 0.0003.
Values sent between devices are 32-bit elements; how exact they have to be, the bound alone decides.
A program may use at most 32 MiB of HBM per device.

```python
import jax
import jax.numpy as jnp
from jax import lax

WINDOW_ROWS = 128
BLOCK_REFLECTORS = 64
SWEEP_ROUNDS = 4
NR = 8192
NC = 8192
SWEEP_WINDOWS = 64


def reflector_blocks(key):
    vector_key = jax.random.fold_in(key, 0)
    householder_vectors = jax.random.normal(vector_key, (SWEEP_ROUNDS, 2, SWEEP_WINDOWS, BLOCK_REFLECTORS, WINDOW_ROWS), jnp.float32)
    householder_vectors = jnp.clip(householder_vectors, -6.0, 6.0)
    gram = jnp.einsum('abkiw,abkjw->abkij', householder_vectors, householder_vectors, precision=lax.Precision.HIGHEST)
    unit = jnp.eye(BLOCK_REFLECTORS, dtype=jnp.float32)
    inverse = jnp.triu(gram, 1) + 0.5 * gram * unit
    target = jnp.broadcast_to(unit, inverse.shape)
    factor = jax.scipy.linalg.solve_triangular(inverse, target, lower=False)
    return jnp.concatenate([householder_vectors, factor], -1)


def draw_refl(key, part):
    return reflector_blocks(jax.random.fold_in(key, 11))


def draw_offsets(key, part):
    akey, bkey = jax.random.split(jax.random.fold_in(key, 7))
    values = jax.random.randint(akey, (SWEEP_ROUNDS * 2,), 1, 127)
    order = jax.random.permutation(bkey, SWEEP_ROUNDS * 2)
    values = jnp.where(order == 0, 0, jnp.where(order == 1, 127, values))
    return values.reshape(SWEEP_ROUNDS, 2).astype(jnp.int32)


def shard_levels(key, extent, cuts, smallest, largest):
    gain = 1.0
    for dim, blocks in cuts:
        draws = jax.random.uniform(jax.random.fold_in(jax.random.fold_in(key, 6), dim), (blocks,), jnp.float32, smallest / len(cuts), largest / len(cuts))
        gain = gain * jnp.repeat(jnp.exp(draws), extent[dim] // blocks).reshape((-1,) + (1,) * (len(extent) - 1 - dim))
    return gain


def centred(rng, shape, width, bound, pieces=(), kind=jnp.bfloat16):
    drawn = width * jax.random.normal(rng, shape, jnp.float32)
    if pieces:
        drawn = drawn * shard_levels(rng, shape, pieces, -0.22, 0.18)
    return jnp.clip(drawn, -bound, bound).astype(kind)


def setup_inputs(seed: int = 0) -> dict:
    key_list = jax.random.split(jax.random.key(seed), 4)
    return {
        "evecs": centred(key_list[0], (NR, NC), 1.0, 6.0, ((0, 16), (1, 64)), jnp.float32),
        "offsets": draw_offsets(jax.random.fold_in(key_list[3], 71), 0),
        "refl": draw_refl(jax.random.fold_in(key_list[3], 71), 0),
    }


def reference(evecs, offsets, refl):
    rows, cols = evecs.shape
    padded = jnp.concatenate([evecs, jnp.zeros((WINDOW_ROWS, cols), jnp.float32)], 0)
    for rnd in range(SWEEP_ROUNDS):
        for sweep in range(2):
            start = offsets[rnd, sweep]

            def step(index, field):
                first = (start + index * WINDOW_ROWS).astype(jnp.int32)
                window = lax.dynamic_slice_in_dim(field, first, WINDOW_ROWS, 0)
                block = refl[rnd, sweep, index]
                reflect = block[:, :WINDOW_ROWS]
                factor = block[:, WINDOW_ROWS:]
                proj = jnp.dot(reflect, window, precision=lax.Precision.HIGHEST)
                scaled = jnp.dot(factor, proj, precision=lax.Precision.HIGHEST)
                window = window - jnp.dot(reflect.T, scaled, precision=lax.Precision.HIGHEST)
                return lax.dynamic_update_slice_in_dim(field, window, first, 0)
            padded = lax.fori_loop(0, SWEEP_WINDOWS, step, padded)
            padded = jnp.concatenate([padded[:rows], jnp.zeros((WINDOW_ROWS, cols), jnp.float32)], 0)
    return padded[:rows]
```

```python
import functools

import jax
import jax.numpy as jnp
from jax import lax
from jax.experimental import pallas as pl
from jax.experimental.pallas import tpu as pltpu
from jax.sharding import PartitionSpec as P

WR = 128
NREF = 64
ROUNDS = 4
NWIN = 4
NCOL = 128
STRIDE = 2
CHUNKS = 2
CROWS = 24
SROWS = CHUNKS * CROWS
MESH = pl.DeviceIdType.MESH
F32 = jnp.float32
BF16 = jnp.bfloat16


def split(x):
    hi = x.astype(BF16)
    return hi, (x - hi.astype(F32)).astype(BF16)


def dot3(a, b, dims):
    def one(x, y):
        return lax.dot_general(x, y, (dims, ((), ())), preferred_element_type=F32)

    (ah, al), (bh, bl) = a, b
    return one(ah, bh) + (one(ah, bl) + one(al, bh))


def kernel(
    nrow, nz, off_ref, refl_ref, ev_ref, out_ref,
    gath, own0, own1, lo0, lo1, hi0, hi1, hmat_hi, hmat_lo,
    zsend, zrecv, psend, precv, xsend, xrecv, lsem,
):
    p = lax.axis_index("row")
    j = lax.axis_index("col")
    z, c = j // 2, j % 2
    partner = z * 2 + (1 - c)
    own, lo, hi = (own0, own1), (lo0, lo1), (hi0, hi1)

    def chip(d):
        return lax.rem(z + d + 2 * nz, nz)

    barrier = pltpu.get_barrier_semaphore()
    for d in [x for x in range(-STRIDE, STRIDE + 1) if x]:
        pl.semaphore_signal(barrier, inc=1, device_id={"col": chip(d) * 2 + c}, device_id_type=MESH)
    pl.semaphore_signal(barrier, inc=1, device_id={"col": partner}, device_id_type=MESH)

    @pl.when(p > 0)
    def _():
        pl.semaphore_signal(barrier, inc=1, device_id={"row": p - 1}, device_id_type=MESH)

    @pl.when(p < nrow - 1)
    def _():
        pl.semaphore_signal(barrier, inc=1, device_id={"row": p + 1}, device_id_type=MESH)

    local = [
        pltpu.make_async_copy(ev_ref, own0, lsem.at[0]),
        pltpu.make_async_copy(ev_ref.at[pl.ds(0, 2 * WR)], lo0.at[pl.ds(2 * WR, 2 * WR)], lsem.at[1]),
        pltpu.make_async_copy(ev_ref.at[pl.ds(2 * WR, 2 * WR)], hi0.at[pl.ds(0, 2 * WR)], lsem.at[2]),
    ]
    for copy in local:
        copy.start()

    def piece(rnd):
        return refl_ref[pl.ds(8 * rnd, 8), :WR]

    def factors(rnd):
        a = refl_ref[pl.ds(8 * rnd, 8), WR:]
        b = refl_ref[pl.ds(8 * rnd + 8, 8), WR:]
        return jnp.concatenate([a, b], 1)

    base = pl.multiple_of(j * SROWS, 8)
    for tile, value in enumerate((piece(0), factors(0), piece(1), piece(2), factors(2), piece(3))):
        gath[pl.ds(base + 8 * tile, 8), :value.shape[1]] = value
    for par in range(2):
        lo[par][pl.ds(0, WR), :] = jnp.zeros((WR, NCOL), F32)

    @pl.when(p == 0)
    def _():
        for par in range(2):
            lo[par][pl.ds(WR, WR), :] = jnp.zeros((WR, NCOL), F32)

    @pl.when(p == nrow - 1)
    def _():
        for par in range(2):
            hi[par][pl.ds(2 * WR, WR), :] = jnp.zeros((WR, NCOL), F32)

    pl.semaphore_wait(barrier, 2 * STRIDE + 1 + (p > 0).astype(jnp.int32) + (p < nrow - 1).astype(jnp.int32))

    def down(t):
        par = t % 2
        src = ev_ref.at[pl.ds(0, WR)] if t == 0 else lo[par].at[pl.ds(2 * WR, WR)]
        return pltpu.make_async_remote_copy(
            src, hi[par].at[pl.ds(2 * WR, WR)], xsend.at[0, par], xrecv.at[0, par],
            device_id={"row": p - 1}, device_id_type=MESH,
        )

    def up(t):
        par = t % 2
        return pltpu.make_async_remote_copy(
            hi[par].at[pl.ds(WR, WR)], lo[par].at[pl.ds(WR, WR)], xsend.at[1, par], xrecv.at[1, par],
            device_id={"row": p + 1}, device_id_type=MESH,
        )

    def if_below(f):
        pl.when(p > 0)(f)

    def if_above(f):
        pl.when(p < nrow - 1)(f)

    if_below(lambda: down(0).start())

    def rows_of(chip_index, core, q):
        at = (chip_index * 2 + core) * SROWS + q * CROWS
        return gath.at[pl.ds(pl.multiple_of(at, 8), CROWS)]

    def hop(way, d, q, reach):
        sgn = 1 - 2 * way
        part = rows_of(chip(-sgn * d), c, q)
        return pltpu.make_async_remote_copy(
            part, part, zsend.at[way, q, d + reach], zrecv.at[way, q, d + reach],
            device_id={"col": chip(sgn * reach) * 2 + c}, device_id_type=MESH,
        )

    def arrival(way, d, q):
        sgn = 1 - 2 * way
        part = rows_of(chip(-sgn * d), c, q)
        return pltpu.make_async_remote_copy(
            part, part, zsend.at[way, q, d], zrecv.at[way, q, d],
            device_id={"col": chip(sgn) * 2 + c}, device_id_type=MESH,
        )

    def across(src_chip, q):
        part = rows_of(src_chip, c, q)
        return pltpu.make_async_remote_copy(
            part, part, psend.at[q, src_chip], precv.at[q, src_chip],
            device_id={"col": partner}, device_id_type=MESH,
        )

    def from_partner(src_chip, q):
        part = rows_of(src_chip, 1 - c, q)
        return pltpu.make_async_remote_copy(
            part, part, psend.at[q, src_chip], precv.at[q, src_chip],
            device_id={"col": partner}, device_id_type=MESH,
        )

    def far(way, q):
        return nz // 2 if way == q else nz // 2 - 1

    def reaches(d, way, q, last):
        order = [STRIDE] + list(range(1, STRIDE))
        return [r for r in order if not last or d + r <= far(way, q)]

    def relay(d, last):
        for q in range(CHUNKS):
            for way in range(2):
                if not isinstance(d, int) or d > 0:
                    arrival(way, d, q).wait_recv()
                for r in reaches(d, way, q, last):
                    hop(way, d, q, r).start()
            if isinstance(d, int) and d == 0:
                across(z, q).start()
            else:
                for way in range(2):
                    across(chip((2 * way - 1) * d), q).start()

    def settle_step(d):
        for q in range(CHUNKS):
            for way in range(2):
                for r in range(1, STRIDE):
                    arrival(way, d + r, q).wait_recv()
                    across(chip((2 * way - 1) * (d + r)), q).start()

    half = nz // 2
    last_relay = half - STRIDE
    relay(0, last_relay == 0)

    def step(m, carry):
        relay(m * STRIDE, False)
        settle_step((m - 1) * STRIDE)
        return carry

    lax.fori_loop(1, last_relay // STRIDE, step, 0)
    relay(last_relay, True)
    if last_relay:
        settle_step(last_relay - STRIDE)
    for q in range(CHUNKS):
        for way in range(2):
            for d in range(last_relay + 1, far(way, q) + 1):
                arrival(way, d, q).wait_recv()
                across(chip((2 * way - 1) * d), q).start()

    def partner_done(q):
        def body(i, carry):
            from_partner(i, q).wait_recv()
            return carry
        lax.fori_loop(0, nz, body, 0)

    for copy in local:
        copy.wait()

    eye = (
        lax.broadcasted_iota(jnp.int32, (WR, WR), 0) == lax.broadcasted_iota(jnp.int32, (WR, WR), 1)
    ).astype(F32)

    def build(t):
        rnd, sweep = t // 2, t % 2
        vtile = (0, 2, 3, 5)[rnd]
        ttile = (1, 1, 4, 4)[rnd]
        for w in range(NWIN):
            row = sweep * NWIN + w
            vt = split(gath[pl.ds(8 * vtile + row, NREF, stride=SROWS), :])
            packed = gath[pl.ds(8 * ttile + row, NREF, stride=SROWS), :]
            tf = split(packed[:, NREF * (rnd % 2):NREF * (rnd % 2) + NREF])
            tv = split(dot3(tf, vt, ((1,), (0,))))
            h, l = split(eye - dot3(vt, tv, ((0,), (0,))))
            hmat_hi[t % 2, w] = h
            hmat_lo[t % 2, w] = l

    def apply(t, w, rows):
        e = split(rows)
        return dot3((hmat_hi[t % 2, w], hmat_lo[t % 2, w]), e, ((1,), (0,)))

    def offset(t):
        return off_ref[(t - 1) // 2, (t - 1) % 2] if t else 0

    lines = lax.broadcasted_iota(jnp.int32, (WR, NCOL), 0)
    partner_done(0)
    build(0)
    for t in range(1, 2 * ROUNDS + 1):
        old, new = (t - 1) % 2, t % 2
        shift = offset(t) - offset(t - 1)
        for w in (1, 2):
            got = apply(t - 1, w, own[old][pl.ds(shift + WR * w, WR), :])
            own[new][pl.ds(WR * w, WR), :] = got
            if w == 1:
                lo[new][pl.ds(3 * WR, WR), :] = got
            else:
                hi[new][pl.ds(0, WR), :] = got
        if t == ROUNDS:
            partner_done(1)
        if t < 2 * ROUNDS:
            build(t)
        if_above(lambda: down(t - 1).wait_recv())
        if t > 1:
            if_below(lambda: up(t - 1).wait_recv())
        if t > 2:
            if_below(lambda: down(t - 2).wait_send())
            if_above(lambda: up(t - 2).wait_send())
        elif t == 2:
            if_below(lambda: down(0).wait_send())

        @pl.when(p == 0)
        def _():
            lo[new][pl.ds(WR, WR), :] = lo[old][pl.ds(shift + WR, WR), :]

        got = apply(t - 1, 0, lo[old][pl.ds(shift + 2 * WR, WR), :])
        lo[new][pl.ds(2 * WR, WR), :] = got
        if t < 2 * ROUNDS:
            if_below(lambda: down(t).start())
        own[new][pl.ds(0, WR), :] = got
        got = apply(t - 1, 3, hi[old][pl.ds(shift + WR, WR), :])
        limit = jnp.where(p == nrow - 1, WR - offset(t), WR)
        got = jnp.where(lines < limit, got, 0.0)
        hi[new][pl.ds(WR, WR), :] = got
        if_above(lambda: up(t).start())
        own[new][pl.ds(3 * WR, WR), :] = got

    final = 2 * ROUNDS
    par = final % 2
    tail = pltpu.make_async_copy(own[par], out_ref.at[pl.ds(WR, NWIN * WR)], lsem.at[0])
    tail.start()
    if_below(lambda: up(final).wait_recv())
    head = pltpu.make_async_copy(lo[par].at[pl.ds(WR, WR)], out_ref.at[pl.ds(0, WR)], lsem.at[1])
    head.start()

    if_below(lambda: down(final - 1).wait_send())
    if_above(lambda: up(final - 1).wait_send())
    if_above(lambda: up(final).wait_send())

    def drain(i, carry):
        for q in range(CHUNKS):
            across(i, q).wait_send()
        return carry

    lax.fori_loop(0, nz, drain, 0)
    for q in range(CHUNKS):
        for way in range(2):
            def drain_z(d, carry, way=way, q=q):
                arrival(way, d, q).wait_send()
                return carry
            lax.fori_loop(1, far(way, q) + 1, drain_z, 0)
    tail.wait()
    head.wait()


def shards(evecs, offsets, refl):
    nrow, ncol = lax.axis_size("row"), lax.axis_size("col")
    nz = ncol // 2
    vec = lambda rows: pltpu.VMEM((rows, NCOL), F32)
    sem = pltpu.SemaphoreType.DMA
    reach = nz // 2 + 1
    spread = pl.pallas_call(
        functools.partial(kernel, nrow, nz),
        out_shape=jax.ShapeDtypeStruct(((NWIN + 1) * WR, NCOL), F32),
        in_specs=[
            pl.BlockSpec(memory_space=pltpu.SMEM),
            pl.BlockSpec(memory_space=pltpu.VMEM),
            pl.BlockSpec(memory_space=pl.ANY),
        ],
        out_specs=pl.BlockSpec(memory_space=pl.ANY),
        scratch_shapes=[
            vec(ncol * SROWS),
            vec(NWIN * WR), vec(NWIN * WR), vec(4 * WR), vec(4 * WR), vec(3 * WR), vec(3 * WR),
            pltpu.VMEM((2, NWIN, WR, WR), BF16), pltpu.VMEM((2, NWIN, WR, WR), BF16),
            sem((2, CHUNKS, reach)), sem((2, CHUNKS, reach)),
            sem((CHUNKS, nz)), sem((CHUNKS, nz)),
            sem((2, 2)), sem((2, 2)), sem((3,)),
        ],
        compiler_params=pltpu.CompilerParams(collective_id=0, has_side_effects=True),
        name="sweeps",
    )(offsets, refl.reshape(ROUNDS * 2 * NWIN, WR + NREF), evecs)
    start = WR - offsets[ROUNDS - 1, 1]
    return lax.dynamic_slice_in_dim(spread, start, NWIN * WR, 0)


def solution(mesh):
    placed = (P("row", "col"), P(), P(None, None, "row", "col", None))
    return jax.shard_map(
        shards, mesh=mesh, in_specs=placed, out_specs=P("row", "col"), check_vma=False
    )
```

```python
import functools

import jax
import jax.numpy as jnp
from jax import lax
from jax.experimental import pallas as pl
from jax.experimental.pallas import tpu as pltpu
from jax.sharding import PartitionSpec as P

WR = 128
NREF = 64
ROUNDS = 4
NWIN = 4
NCOL = 128
STRIDE = 4
CHUNKS = 2
CROWS = 24
SROWS = CHUNKS * CROWS
MESH = pl.DeviceIdType.MESH
F32 = jnp.float32
BF16 = jnp.bfloat16


def split(x):
    hi = x.astype(BF16)
    return hi, (x - hi.astype(F32)).astype(BF16)


def dot3(a, b, dims):
    def one(x, y):
        return lax.dot_general(x, y, (dims, ((), ())), preferred_element_type=F32)

    (ah, al), (bh, bl) = a, b
    return one(ah, bh) + (one(ah, bl) + one(al, bh))


def kernel(
    nrow, nz, off_hbm, refl_ref, ev_ref, out_ref,
    gath, own0, own1, lo0, lo1, hi0, hi1, hmat_hi, hmat_lo,
    zsend, zrecv, psend, precv, xsend, xrecv, lsem, off_ref,
):
    p = lax.axis_index("row")
    j = lax.axis_index("col")
    z, c = j // 2, j % 2
    partner = z * 2 + (1 - c)
    own, lo, hi = (own0, own1), (lo0, lo1), (hi0, hi1)

    def chip(d):
        return lax.rem(z + d + 2 * nz, nz)

    barrier = pltpu.get_barrier_semaphore()
    for d in [x for x in range(-STRIDE, STRIDE + 1) if x]:
        pl.semaphore_signal(barrier, inc=1, device_id={"col": chip(d) * 2 + c}, device_id_type=MESH)
    pl.semaphore_signal(barrier, inc=1, device_id={"col": partner}, device_id_type=MESH)

    @pl.when(p > 0)
    def _():
        pl.semaphore_signal(barrier, inc=1, device_id={"row": p - 1}, device_id_type=MESH)

    @pl.when(p < nrow - 1)
    def _():
        pl.semaphore_signal(barrier, inc=1, device_id={"row": p + 1}, device_id_type=MESH)

    local = [
        pltpu.make_async_copy(ev_ref, own0, lsem.at[0]),
        pltpu.make_async_copy(ev_ref.at[pl.ds(0, 2 * WR)], lo0.at[pl.ds(2 * WR, 2 * WR)], lsem.at[1]),
        pltpu.make_async_copy(ev_ref.at[pl.ds(2 * WR, 2 * WR)], hi0.at[pl.ds(0, 2 * WR)], lsem.at[2]),
        pltpu.make_async_copy(off_hbm, off_ref, lsem.at[3]),
    ]
    for copy in local:
        copy.start()

    def shard_rows(rnd, lanes):
        return jnp.concatenate(
            [refl_ref[rnd, sweep, w, :, lanes] for sweep in range(2) for w in range(NWIN)], 0
        )

    def piece(rnd):
        return shard_rows(rnd, slice(0, WR))

    def factors(rnd):
        lanes = slice(WR, WR + NREF)
        return jnp.concatenate([shard_rows(rnd, lanes), shard_rows(rnd + 1, lanes)], 1)

    base = pl.multiple_of(j * SROWS, 8)
    for tile, value in enumerate((piece(0), factors(0), piece(1), piece(2), factors(2), piece(3))):
        gath[pl.ds(base + 8 * tile, 8), :value.shape[1]] = value
    for par in range(2):
        lo[par][pl.ds(0, WR), :] = jnp.zeros((WR, NCOL), F32)

    @pl.when(p == 0)
    def _():
        for par in range(2):
            lo[par][pl.ds(WR, WR), :] = jnp.zeros((WR, NCOL), F32)

    @pl.when(p == nrow - 1)
    def _():
        for par in range(2):
            hi[par][pl.ds(2 * WR, WR), :] = jnp.zeros((WR, NCOL), F32)

    pl.semaphore_wait(barrier, 2 * STRIDE + 1 + (p > 0).astype(jnp.int32) + (p < nrow - 1).astype(jnp.int32))

    def down(t):
        par = t % 2
        src = ev_ref.at[pl.ds(0, WR)] if t == 0 else lo[par].at[pl.ds(2 * WR, WR)]
        return pltpu.make_async_remote_copy(
            src, hi[par].at[pl.ds(2 * WR, WR)], xsend.at[0, par], xrecv.at[0, par],
            device_id={"row": p - 1}, device_id_type=MESH,
        )

    def up(t):
        par = t % 2
        return pltpu.make_async_remote_copy(
            hi[par].at[pl.ds(WR, WR)], lo[par].at[pl.ds(WR, WR)], xsend.at[1, par], xrecv.at[1, par],
            device_id={"row": p + 1}, device_id_type=MESH,
        )

    def if_below(f):
        pl.when(p > 0)(f)

    def if_above(f):
        pl.when(p < nrow - 1)(f)

    if_below(lambda: down(0).start())

    def rows_of(chip_index, core, q):
        at = (chip_index * 2 + core) * SROWS + q * CROWS
        return gath.at[pl.ds(pl.multiple_of(at, 8), CROWS)]

    def hop(way, d, q, reach):
        sgn = 1 - 2 * way
        part = rows_of(chip(-sgn * d), c, q)
        return pltpu.make_async_remote_copy(
            part, part, zsend.at[way, q, d + reach], zrecv.at[way, q, d + reach],
            device_id={"col": chip(sgn * reach) * 2 + c}, device_id_type=MESH,
        )

    def arrival(way, d, q):
        sgn = 1 - 2 * way
        part = rows_of(chip(-sgn * d), c, q)
        return pltpu.make_async_remote_copy(
            part, part, zsend.at[way, q, d], zrecv.at[way, q, d],
            device_id={"col": chip(sgn) * 2 + c}, device_id_type=MESH,
        )

    def across(src_chip, q):
        part = rows_of(src_chip, c, q)
        return pltpu.make_async_remote_copy(
            part, part, psend.at[q, src_chip], precv.at[q, src_chip],
            device_id={"col": partner}, device_id_type=MESH,
        )

    def from_partner(src_chip, q):
        part = rows_of(src_chip, 1 - c, q)
        return pltpu.make_async_remote_copy(
            part, part, psend.at[q, src_chip], precv.at[q, src_chip],
            device_id={"col": partner}, device_id_type=MESH,
        )

    def far(way, q):
        return nz // 2 if way == q else nz // 2 - 1

    def relay(d, q):
        for way in range(2):
            if d:
                arrival(way, d, q).wait_recv()
            for r in [STRIDE] + list(range(1, STRIDE)):
                if d + r <= far(way, q):
                    hop(way, d, q, r).start()
        for way in range(2 if d else 1):
            across(chip((2 * way - 1) * d), q).start()

    def settle(first, q):
        for way in range(2):
            for d in range(first, first + STRIDE):
                if d % STRIDE and d <= far(way, q) or d == nz // 2 == far(way, q):
                    arrival(way, d, q).wait_recv()
                    across(chip((2 * way - 1) * d), q).start()

    relays = range(0, nz // 2, STRIDE)

    def steps_of(q):
        steps = []
        for d in relays:
            steps.append([functools.partial(relay, d, q)])
            if d:
                steps[-1].append(functools.partial(settle, d - STRIDE + 1, q))
        steps.append([functools.partial(settle, relays[-1] + 1, q)])
        return steps

    early, late = steps_of(0), steps_of(1)

    def run(step):
        for part in step:
            part()

    behind = len(early) - 3
    for i, step in enumerate(early):
        step[0]()
        if 0 <= i - behind and i < len(early) - 1:
            late.pop(0)[0]() if i == behind else run(late.pop(0))
        for part in step[1:]:
            part()

    def partner_done(q):
        def body(i, carry):
            from_partner(i, q).wait_recv()
            return carry
        lax.fori_loop(0, nz, body, 0)

    for copy in local:
        copy.wait()

    eye = (
        lax.broadcasted_iota(jnp.int32, (WR, WR), 0) == lax.broadcasted_iota(jnp.int32, (WR, WR), 1)
    ).astype(F32)

    def build(t):
        rnd, sweep = t // 2, t % 2
        vtile = (0, 2, 3, 5)[rnd]
        ttile = (1, 1, 4, 4)[rnd]
        for w in range(NWIN):
            row = sweep * NWIN + w
            vt = split(gath[pl.ds(8 * vtile + row, NREF, stride=SROWS), :])
            packed = gath[pl.ds(8 * ttile + row, NREF, stride=SROWS), :]
            tf = split(packed[:, NREF * (rnd % 2):NREF * (rnd % 2) + NREF])
            tv = split(dot3(tf, vt, ((1,), (0,))))
            h, l = split(eye - dot3(vt, tv, ((0,), (0,))))
            hmat_hi[t % 2, w] = h
            hmat_lo[t % 2, w] = l

    def apply(t, w, rows):
        e = split(rows)
        return dot3((hmat_hi[t % 2, w], hmat_lo[t % 2, w]), e, ((1,), (0,)))

    def offset(t):
        return off_ref[(t - 1) % 2, (t - 1) // 2] if t else 0

    lines = lax.broadcasted_iota(jnp.int32, (WR, NCOL), 0)
    partner_done(0)
    build(0)
    for t in range(1, 2 * ROUNDS + 1):
        old, new = (t - 1) % 2, t % 2
        shift = offset(t) - offset(t - 1)
        for w in (1, 2):
            got = apply(t - 1, w, own[old][pl.ds(shift + WR * w, WR), :])
            own[new][pl.ds(WR * w, WR), :] = got
            if w == 1:
                lo[new][pl.ds(3 * WR, WR), :] = got
            else:
                hi[new][pl.ds(0, WR), :] = got
        if late:
            run(late.pop(0))
        if t == ROUNDS:
            partner_done(1)
        if t < 2 * ROUNDS:
            build(t)
        if_above(lambda: down(t - 1).wait_recv())
        if t > 1:
            if_below(lambda: up(t - 1).wait_recv())
        if t > 2:
            if_below(lambda: down(t - 2).wait_send())
            if_above(lambda: up(t - 2).wait_send())
        elif t == 2:
            if_below(lambda: down(0).wait_send())

        @pl.when(p == 0)
        def _():
            lo[new][pl.ds(WR, WR), :] = lo[old][pl.ds(shift + WR, WR), :]

        got = apply(t - 1, 0, lo[old][pl.ds(shift + 2 * WR, WR), :])
        lo[new][pl.ds(2 * WR, WR), :] = got
        if t < 2 * ROUNDS:
            if_below(lambda: down(t).start())
        own[new][pl.ds(0, WR), :] = got
        got = apply(t - 1, 3, hi[old][pl.ds(shift + WR, WR), :])
        limit = jnp.where(p == nrow - 1, WR - offset(t), WR)
        got = jnp.where(lines < limit, got, 0.0)
        hi[new][pl.ds(WR, WR), :] = got
        if_above(lambda: up(t).start())
        own[new][pl.ds(3 * WR, WR), :] = got

    final = 2 * ROUNDS
    par = final % 2
    result = own[1 - par]
    result[pl.ds(WR, 3 * WR), :] = own[par][pl.ds(WR - offset(final), 3 * WR), :]
    tail = pltpu.make_async_copy(
        result.at[pl.ds(WR, 3 * WR)], out_ref.at[pl.ds(WR, 3 * WR)], lsem.at[0]
    )
    tail.start()
    if_below(lambda: up(final).wait_recv())
    result[pl.ds(0, WR), :] = lo[par][pl.ds(2 * WR - offset(final), WR), :]
    head = pltpu.make_async_copy(result.at[pl.ds(0, WR)], out_ref.at[pl.ds(0, WR)], lsem.at[1])
    head.start()

    if_below(lambda: down(final - 1).wait_send())
    if_above(lambda: up(final - 1).wait_send())
    if_above(lambda: up(final).wait_send())

    def drain(i, carry):
        for q in range(CHUNKS):
            across(i, q).wait_send()
        return carry

    lax.fori_loop(0, nz, drain, 0)
    for q in range(CHUNKS):
        for way in range(2):
            def drain_z(d, carry, way=way, q=q):
                arrival(way, d, q).wait_send()
                return carry
            lax.fori_loop(1, far(way, q) + 1, drain_z, 0)
    tail.wait()
    head.wait()


def shards(evecs, offsets, refl):
    nrow, ncol = lax.axis_size("row"), lax.axis_size("col")
    nz = ncol // 2
    vec = lambda rows: pltpu.VMEM((rows, NCOL), F32)
    sem = pltpu.SemaphoreType.DMA
    reach = nz // 2 + 1
    return pl.pallas_call(
        functools.partial(kernel, nrow, nz),
        out_shape=jax.ShapeDtypeStruct((NWIN * WR, NCOL), F32),
        in_specs=[
            pl.BlockSpec(memory_space=pl.ANY),
            pl.BlockSpec(memory_space=pltpu.VMEM),
            pl.BlockSpec(memory_space=pl.ANY),
        ],
        out_specs=pl.BlockSpec(memory_space=pl.ANY),
        scratch_shapes=[
            vec(ncol * SROWS),
            vec(NWIN * WR), vec(NWIN * WR), vec(4 * WR), vec(4 * WR), vec(3 * WR), vec(3 * WR),
            pltpu.VMEM((2, NWIN, WR, WR), BF16), pltpu.VMEM((2, NWIN, WR, WR), BF16),
            sem((2, CHUNKS, reach)), sem((2, CHUNKS, reach)),
            sem((CHUNKS, nz)), sem((CHUNKS, nz)),
            sem((2, 2)), sem((2, 2)), sem((4,)),
            pltpu.SMEM((2, ROUNDS), jnp.int32),
        ],
        compiler_params=pltpu.CompilerParams(collective_id=0, has_side_effects=True),
        name="sweeps",
    )(offsets.T, refl, evecs)


def solution(mesh):
    placed = (P("row", "col"), P(), P(None, None, "row", "col", None))
    return jax.shard_map(
        shards, mesh=mesh, in_specs=placed, out_specs=P("row", "col"), check_vma=False
    )
```

```python
import functools

import jax
import jax.numpy as jnp
from jax import lax
from jax.experimental import pallas as pl
from jax.experimental.pallas import tpu as pltpu
from jax.sharding import PartitionSpec as P

WR = 128
NREF = 64
ROUNDS = 4
NWIN = 4
NCOL = 128
OWN = NWIN * WR
BELOW = 3 * WR
STRIDE = 4
CHUNKS = 2
CROWS = 24
SROWS = CHUNKS * CROWS
MESH = pl.DeviceIdType.MESH
F32 = jnp.float32
BF16 = jnp.bfloat16


def split(x):
    hi = x.astype(BF16)
    return hi, (x - hi.astype(F32)).astype(BF16)


def dot3(a, b, dims):
    def one(x, y):
        return lax.dot_general(x, y, (dims, ((), ())), preferred_element_type=F32)

    (ah, al), (bh, bl) = a, b
    return one(ah, bh) + (one(ah, bl) + one(al, bh))


def kernel(
    nrow, nz, off_hbm, refl_ref, ev_ref, out_ref,
    gath, state0, state1, mid, last, sent, got, first_hi, first_lo, second_hi, second_lo,
    zsend, zrecv, psend, precv, xsend, xrecv, hsend, hrecv, lsem, off_ref,
):
    p = lax.axis_index("row")
    j = lax.axis_index("col")
    z, c = j // 2, j % 2
    partner = z * 2 + (1 - c)
    state = (state0, state1)

    def chip(d):
        return lax.rem(z + d + 2 * nz, nz)

    barrier = pltpu.get_barrier_semaphore()
    for d in [x for x in range(-STRIDE, STRIDE + 1) if x]:
        pl.semaphore_signal(barrier, inc=1, device_id={"col": chip(d) * 2 + c}, device_id_type=MESH)
    pl.semaphore_signal(barrier, inc=1, device_id={"col": partner}, device_id_type=MESH)

    @pl.when(p > 0)
    def _():
        pl.semaphore_signal(barrier, inc=1, device_id={"row": p - 1}, device_id_type=MESH)

    @pl.when(p < nrow - 1)
    def _():
        pl.semaphore_signal(barrier, inc=1, device_id={"row": p + 1}, device_id_type=MESH)

    local = [
        pltpu.make_async_copy(ev_ref, state0.at[pl.ds(BELOW, OWN)], lsem.at[0]),
        pltpu.make_async_copy(off_hbm, off_ref, lsem.at[1]),
    ]
    for copy in local:
        copy.start()

    def shard_rows(rnd, lanes):
        return jnp.concatenate(
            [refl_ref[rnd, sweep, w, :, lanes] for sweep in range(2) for w in range(NWIN)], 0
        )

    def piece(rnd):
        return shard_rows(rnd, slice(0, WR))

    def factors(rnd):
        lanes = slice(WR, WR + NREF)
        return jnp.concatenate([shard_rows(rnd, lanes), shard_rows(rnd + 1, lanes)], 1)

    base = pl.multiple_of(j * SROWS, 8)
    for tile, value in enumerate((piece(0), factors(0), piece(1), piece(2), factors(2), piece(3))):
        gath[pl.ds(base + 8 * tile, 8), :value.shape[1]] = value
    eye = (
        lax.broadcasted_iota(jnp.int32, (WR, WR), 0) == lax.broadcasted_iota(jnp.int32, (WR, WR), 1)
    ).astype(F32)

    for par in range(2):
        state[par][pl.ds(0, WR), :] = jnp.zeros((WR, NCOL), F32)

    @pl.when(p == 0)
    def _():
        for par in range(2):
            state[par][pl.ds(WR, 2 * WR), :] = jnp.zeros((2 * WR, NCOL), F32)
        for rnd in range(ROUNDS):
            got[rnd, 0] = eye

    @pl.when(p == nrow - 1)
    def _():
        for par in range(2):
            state[par][pl.ds(BELOW + OWN, 2 * WR), :] = jnp.zeros((2 * WR, NCOL), F32)
        for rnd in range(ROUNDS):
            got[rnd, 1] = eye

    pl.semaphore_wait(barrier, 2 * STRIDE + 1 + (p > 0).astype(jnp.int32) + (p < nrow - 1).astype(jnp.int32))

    def down(r):
        par = r % 2
        src = ev_ref.at[pl.ds(0, 2 * WR)] if r == 0 else state[par].at[pl.ds(BELOW, 2 * WR)]
        return pltpu.make_async_remote_copy(
            src, state[par].at[pl.ds(BELOW + OWN, 2 * WR)], xsend.at[0, par], xrecv.at[0, par],
            device_id={"row": p - 1}, device_id_type=MESH,
        )

    def up(r):
        par = r % 2
        size = WR if r == ROUNDS else 2 * WR
        at = BELOW + OWN - size
        src = ev_ref.at[pl.ds(OWN - size, size)] if r == 0 else state[par].at[pl.ds(at, size)]
        return pltpu.make_async_remote_copy(
            src, state[par].at[pl.ds(BELOW - size, size)], xsend.at[1, par], xrecv.at[1, par],
            device_id={"row": p + 1}, device_id_type=MESH,
        )

    def share(rnd, side):
        return pltpu.make_async_remote_copy(
            sent.at[rnd, side], got.at[rnd, side], hsend.at[rnd, side], hrecv.at[rnd, side],
            device_id={"row": p - 1 if side else p + 1}, device_id_type=MESH,
        )

    def if_below(f):
        pl.when(p > 0)(f)

    def if_above(f):
        pl.when(p < nrow - 1)(f)

    if_below(lambda: down(0).start())
    if_above(lambda: up(0).start())

    def rows_of(chip_index, core, q):
        at = (chip_index * 2 + core) * SROWS + q * CROWS
        return gath.at[pl.ds(pl.multiple_of(at, 8), CROWS)]

    def hop(way, d, q, reach):
        sgn = 1 - 2 * way
        part = rows_of(chip(-sgn * d), c, q)
        return pltpu.make_async_remote_copy(
            part, part, zsend.at[way, q, d + reach], zrecv.at[way, q, d + reach],
            device_id={"col": chip(sgn * reach) * 2 + c}, device_id_type=MESH,
        )

    def arrival(way, d, q):
        sgn = 1 - 2 * way
        part = rows_of(chip(-sgn * d), c, q)
        return pltpu.make_async_remote_copy(
            part, part, zsend.at[way, q, d], zrecv.at[way, q, d],
            device_id={"col": chip(sgn) * 2 + c}, device_id_type=MESH,
        )

    def across(src_chip, q):
        part = rows_of(src_chip, c, q)
        return pltpu.make_async_remote_copy(
            part, part, psend.at[q, src_chip], precv.at[q, src_chip],
            device_id={"col": partner}, device_id_type=MESH,
        )

    def from_partner(src_chip, q):
        part = rows_of(src_chip, 1 - c, q)
        return pltpu.make_async_remote_copy(
            part, part, psend.at[q, src_chip], precv.at[q, src_chip],
            device_id={"col": partner}, device_id_type=MESH,
        )

    def far(way, q):
        return nz // 2 if way == q else nz // 2 - 1

    def relay(d, q):
        for way in range(2):
            if d:
                arrival(way, d, q).wait_recv()
            for r in [STRIDE] + list(range(1, STRIDE)):
                if d + r <= far(way, q):
                    hop(way, d, q, r).start()
        for way in range(2 if d else 1):
            across(chip((2 * way - 1) * d), q).start()

    def settle(first, q):
        for way in range(2):
            for d in range(first, first + STRIDE):
                if d % STRIDE and d <= far(way, q) or d == nz // 2 == far(way, q):
                    arrival(way, d, q).wait_recv()
                    across(chip((2 * way - 1) * d), q).start()

    relays = range(0, nz // 2, STRIDE)

    def steps_of(q):
        steps = []
        for d in relays:
            steps.append([functools.partial(relay, d, q)])
            if d:
                steps[-1].append(functools.partial(settle, d - STRIDE + 1, q))
        steps.append([functools.partial(settle, relays[-1] + 1, q)])
        return steps

    early, late = steps_of(0), steps_of(1)

    def run(step):
        for part in step:
            part()

    behind = len(early) - 3
    for i, step in enumerate(early):
        step[0]()
        if 0 <= i - behind and i < len(early) - 1:
            late.pop(0)[0]() if i == behind else run(late.pop(0))
        for part in step[1:]:
            part()

    def partner_done(q):
        def body(i, carry):
            from_partner(i, q).wait_recv()
            return carry
        lax.fori_loop(0, nz, body, 0)

    for copy in local:
        copy.wait()

    def window(rnd, sweep, w):
        vtile = (0, 2, 3, 5)[rnd]
        ttile = (1, 1, 4, 4)[rnd]
        row = sweep * NWIN + w
        vt = split(gath[pl.ds(8 * vtile + row, NREF, stride=SROWS), :])
        packed = gath[pl.ds(8 * ttile + row, NREF, stride=SROWS), :]
        tf = split(packed[:, NREF * (rnd % 2):NREF * (rnd % 2) + NREF])
        tv = split(dot3(tf, vt, ((1,), (0,))))
        return eye - dot3(vt, tv, ((0,), (0,)))

    def keep(his, los, at, value):
        his[at], los[at] = split(value)

    def build_outer(rnd):
        sent[rnd, 0] = window(rnd, 0, NWIN - 1)
        if_above(lambda: share(rnd, 0).start())
        sent[rnd, 1] = window(rnd, 0, 0)
        if_below(lambda: share(rnd, 1).start())

    def build(rnd):
        keep(first_hi, first_lo, NWIN, sent[rnd, 0])
        keep(first_hi, first_lo, 1, sent[rnd, 1])
        for w in range(1, NWIN - 1):
            keep(first_hi, first_lo, w + 1, window(rnd, 0, w))
        for w in range(NWIN):
            keep(second_hi, second_lo, w, window(rnd, 1, w))

    def offset(t):
        return off_ref[(t - 1) % 2, (t - 1) // 2] if t else 0

    lines = lax.broadcasted_iota(jnp.int32, (WR, NCOL), 0)
    end = jnp.where(p == nrow - 1, OWN, 2 * OWN)

    partner_done(0)
    build_outer(0)
    build(0)
    build_outer(1)
    for rnd in range(ROUNDS):
        old, new = rnd % 2, (rnd + 1) % 2
        before, a, b = offset(2 * rnd), offset(2 * rnd + 1), offset(2 * rnd + 2)
        extra = (b < a).astype(jnp.int32)
        low = a - WR * extra
        if rnd:
            build(rnd)
            if rnd == 2:
                build_outer(3)
        if_below(lambda: up(rnd).wait_recv())
        if_above(lambda: down(rnd).wait_recv())
        if_below(lambda: share(rnd, 0).wait_recv())
        if_above(lambda: share(rnd, 1).wait_recv())
        keep(first_hi, first_lo, 0, got[rnd, 0])
        keep(first_hi, first_lo, NWIN + 1, got[rnd, 1])

        @pl.when(p == 0)
        def _():
            mid[pl.ds(0, WR), :] = state[old][pl.ds(BELOW - WR + low - before, WR), :]

        for i in range(NWIN + 1):
            e = split(state[old][pl.ds(BELOW + WR * i + low - before, WR), :])
            k = i + 1 - extra
            value = dot3((first_hi[k], first_lo[k]), e, ((1,), (0,)))
            if i >= NWIN - 1:
                value = jnp.where(lines < end - low - WR * i, value, 0.0)
            mid[pl.ds(WR * (i + 1), WR), :] = value
        if rnd:
            if_below(lambda: down(rnd - 1).wait_send())
            if_above(lambda: up(rnd - 1).wait_send())
        for w in (3, 2, 0, 1):
            e = split(mid[pl.ds(WR * (w + 1) + b - low, WR), :])
            value = dot3((second_hi[w], second_lo[w]), e, ((1,), (0,)))
            if w == NWIN - 1:
                value = jnp.where(lines < end - b - WR * w, value, 0.0)
            state[new][pl.ds(BELOW + WR * w, WR), :] = value
            if rnd == ROUNDS - 1:
                last[pl.ds(WR * w, WR), :] = value
            if w == (3 if rnd == ROUNDS - 1 else 2):
                if_above(lambda: up(rnd + 1).start())
        if rnd < ROUNDS - 1:
            if_below(lambda: down(rnd + 1).start())

        @pl.when(p == 0)
        def _():
            state[new][pl.ds(BELOW - WR, WR), :] = mid[pl.ds(b - low, WR), :]

        if rnd == 0:
            while late:
                run(late.pop(0))
        if rnd == 1:
            partner_done(1)
            build_outer(2)

    par = ROUNDS % 2
    result = mid
    shift = BELOW - offset(2 * ROUNDS)
    result[pl.ds(WR, 3 * WR), :] = last[pl.ds(WR - offset(2 * ROUNDS), 3 * WR), :]
    tail = pltpu.make_async_copy(
        result.at[pl.ds(WR, 3 * WR)], out_ref.at[pl.ds(WR, 3 * WR)], lsem.at[0]
    )
    tail.start()
    if_below(lambda: up(ROUNDS).wait_recv())
    result[pl.ds(0, WR), :] = state[par][pl.ds(shift, WR), :]
    head = pltpu.make_async_copy(result.at[pl.ds(0, WR)], out_ref.at[pl.ds(0, WR)], lsem.at[1])
    head.start()

    if_below(lambda: down(ROUNDS - 1).wait_send())
    if_above(lambda: up(ROUNDS - 1).wait_send())
    if_above(lambda: up(ROUNDS).wait_send())
    for rnd in range(ROUNDS):
        if_above(lambda: share(rnd, 0).wait_send())
        if_below(lambda: share(rnd, 1).wait_send())

    def drain(i, carry):
        for q in range(CHUNKS):
            across(i, q).wait_send()
        return carry

    lax.fori_loop(0, nz, drain, 0)
    for q in range(CHUNKS):
        for way in range(2):
            def drain_z(d, carry, way=way, q=q):
                arrival(way, d, q).wait_send()
                return carry
            lax.fori_loop(1, far(way, q) + 1, drain_z, 0)
    tail.wait()
    head.wait()


def shards(evecs, offsets, refl):
    nrow, ncol = lax.axis_size("row"), lax.axis_size("col")
    nz = ncol // 2
    vec = lambda rows: pltpu.VMEM((rows, NCOL), F32)
    sem = pltpu.SemaphoreType.DMA
    reach = nz // 2 + 1
    return pl.pallas_call(
        functools.partial(kernel, nrow, nz),
        out_shape=jax.ShapeDtypeStruct((NWIN * WR, NCOL), F32),
        in_specs=[
            pl.BlockSpec(memory_space=pl.ANY),
            pl.BlockSpec(memory_space=pltpu.VMEM),
            pl.BlockSpec(memory_space=pl.ANY),
        ],
        out_specs=pl.BlockSpec(memory_space=pl.ANY),
        scratch_shapes=[
            vec(ncol * SROWS),
            vec(BELOW + OWN + 2 * WR), vec(BELOW + OWN + 2 * WR), vec((NWIN + 2) * WR), vec(OWN),
            pltpu.VMEM((ROUNDS, 2, WR, WR), F32), pltpu.VMEM((ROUNDS, 2, WR, WR), F32),
            pltpu.VMEM((NWIN + 2, WR, WR), BF16), pltpu.VMEM((NWIN + 2, WR, WR), BF16),
            pltpu.VMEM((NWIN, WR, WR), BF16), pltpu.VMEM((NWIN, WR, WR), BF16),
            sem((2, CHUNKS, reach)), sem((2, CHUNKS, reach)),
            sem((CHUNKS, nz)), sem((CHUNKS, nz)),
            sem((2, 2)), sem((2, 2)), sem((ROUNDS, 2)), sem((ROUNDS, 2)), sem((2,)),
            pltpu.SMEM((2, ROUNDS), jnp.int32),
        ],
        compiler_params=pltpu.CompilerParams(collective_id=0, has_side_effects=True),
        name="sweeps",
    )(offsets.T, refl, evecs)


def solution(mesh):
    placed = (P("row", "col"), P(), P(None, None, "row", "col", None))
    return jax.shard_map(
        shards, mesh=mesh, in_specs=placed, out_specs=P("row", "col"), check_vma=False
    )
```

```python
import functools

import jax
import jax.numpy as jnp
from jax import lax
from jax.experimental import pallas as pl
from jax.experimental.pallas import tpu as pltpu
from jax.sharding import PartitionSpec as P

WR = 128
NREF = 64
ROUNDS = 4
NWIN = 4
NCOL = 128
OWN = NWIN * WR
BELOW = 3 * WR
CHUNKS = 2
STRIDES = (4, 4)
PLAN = (0, 1, 1, 1, 1, 1, 0)
CROWS = 24
SROWS = CHUNKS * CROWS
MESH = pl.DeviceIdType.MESH
F32 = jnp.float32
BF16 = jnp.bfloat16


def split(x):
    hi = x.astype(BF16)
    return hi, (x - hi.astype(F32)).astype(BF16)


def dot3(a, b, dims):
    def one(x, y):
        return lax.dot_general(x, y, (dims, ((), ())), preferred_element_type=F32)

    (ah, al), (bh, bl) = a, b
    return one(ah, bh) + (one(ah, bl) + one(al, bh))


def kernel(
    nrow, nz, off_hbm, refl_ref, ev_ref, out_ref,
    gath, state0, state1, mid, last, sent, got, first_hi, first_lo, second_hi, second_lo,
    zsend, zrecv, psend, precv, xsend, xrecv, hsend, hrecv, lsem, off_ref,
):
    p = lax.axis_index("row")
    j = lax.axis_index("col")
    z, c = j // 2, j % 2
    partner = z * 2 + (1 - c)
    state = (state0, state1)

    def chip(d):
        return lax.rem(z + d + 2 * nz, nz)

    barrier = pltpu.get_barrier_semaphore()
    for d in [x for x in range(-max(STRIDES), max(STRIDES) + 1) if x]:
        pl.semaphore_signal(barrier, inc=1, device_id={"col": chip(d) * 2 + c}, device_id_type=MESH)
    pl.semaphore_signal(barrier, inc=1, device_id={"col": partner}, device_id_type=MESH)

    @pl.when(p > 0)
    def _():
        pl.semaphore_signal(barrier, inc=1, device_id={"row": p - 1}, device_id_type=MESH)

    @pl.when(p < nrow - 1)
    def _():
        pl.semaphore_signal(barrier, inc=1, device_id={"row": p + 1}, device_id_type=MESH)

    local = [
        pltpu.make_async_copy(ev_ref, state0.at[pl.ds(BELOW, OWN)], lsem.at[0]),
        pltpu.make_async_copy(off_hbm, off_ref, lsem.at[1]),
    ]
    for copy in local:
        copy.start()

    def shard_rows(rnd, lanes):
        return jnp.concatenate(
            [refl_ref[rnd, sweep, w, :, lanes] for sweep in range(2) for w in range(NWIN)], 0
        )

    def piece(rnd):
        return shard_rows(rnd, slice(0, WR))

    def factors(rnd):
        lanes = slice(WR, WR + NREF)
        return jnp.concatenate([shard_rows(rnd, lanes), shard_rows(rnd + 1, lanes)], 1)

    base = pl.multiple_of(j * SROWS, 8)
    for tile, value in enumerate((piece(0), factors(0), piece(1), piece(2), factors(2), piece(3))):
        gath[pl.ds(base + 8 * tile, 8), :value.shape[1]] = value
    eye = (
        lax.broadcasted_iota(jnp.int32, (WR, WR), 0) == lax.broadcasted_iota(jnp.int32, (WR, WR), 1)
    ).astype(F32)

    for par in range(2):
        state[par][pl.ds(0, WR), :] = jnp.zeros((WR, NCOL), F32)

    @pl.when(p == 0)
    def _():
        for par in range(2):
            state[par][pl.ds(WR, 2 * WR), :] = jnp.zeros((2 * WR, NCOL), F32)
        for rnd in range(ROUNDS):
            got[rnd, 0] = eye

    @pl.when(p == nrow - 1)
    def _():
        for par in range(2):
            state[par][pl.ds(BELOW + OWN, 2 * WR), :] = jnp.zeros((2 * WR, NCOL), F32)
        for rnd in range(ROUNDS):
            got[rnd, 1] = eye

    pl.semaphore_wait(barrier, 2 * max(STRIDES) + 1 + (p > 0).astype(jnp.int32) + (p < nrow - 1).astype(jnp.int32))

    def down(r):
        par = r % 2
        src = ev_ref.at[pl.ds(0, 2 * WR)] if r == 0 else state[par].at[pl.ds(BELOW, 2 * WR)]
        return pltpu.make_async_remote_copy(
            src, state[par].at[pl.ds(BELOW + OWN, 2 * WR)], xsend.at[0, par], xrecv.at[0, par],
            device_id={"row": p - 1}, device_id_type=MESH,
        )

    def up(r):
        par = r % 2
        size = WR if r == ROUNDS else 2 * WR
        at = BELOW + OWN - size
        src = ev_ref.at[pl.ds(OWN - size, size)] if r == 0 else state[par].at[pl.ds(at, size)]
        return pltpu.make_async_remote_copy(
            src, state[par].at[pl.ds(BELOW - size, size)], xsend.at[1, par], xrecv.at[1, par],
            device_id={"row": p + 1}, device_id_type=MESH,
        )

    def share(rnd, side):
        return pltpu.make_async_remote_copy(
            sent.at[rnd, side], got.at[rnd, side], hsend.at[rnd, side], hrecv.at[rnd, side],
            device_id={"row": p - 1 if side else p + 1}, device_id_type=MESH,
        )

    def if_below(f):
        pl.when(p > 0)(f)

    def if_above(f):
        pl.when(p < nrow - 1)(f)

    if_below(lambda: down(0).start())
    if_above(lambda: up(0).start())

    def rows_of(chip_index, core, q):
        at = (chip_index * 2 + core) * SROWS + q * CROWS
        return gath.at[pl.ds(pl.multiple_of(at, 8), CROWS)]

    def hop(way, d, q, reach):
        sgn = 1 - 2 * way
        part = rows_of(chip(-sgn * d), c, q)
        return pltpu.make_async_remote_copy(
            part, part, zsend.at[way, q, d + reach], zrecv.at[way, q, d + reach],
            device_id={"col": chip(sgn * reach) * 2 + c}, device_id_type=MESH,
        )

    def arrival(way, d, q):
        sgn = 1 - 2 * way
        part = rows_of(chip(-sgn * d), c, q)
        return pltpu.make_async_remote_copy(
            part, part, zsend.at[way, q, d], zrecv.at[way, q, d],
            device_id={"col": chip(sgn) * 2 + c}, device_id_type=MESH,
        )

    def across(src_chip, q):
        part = rows_of(src_chip, c, q)
        return pltpu.make_async_remote_copy(
            part, part, psend.at[q, src_chip], precv.at[q, src_chip],
            device_id={"col": partner}, device_id_type=MESH,
        )

    def from_partner(src_chip, q):
        part = rows_of(src_chip, 1 - c, q)
        return pltpu.make_async_remote_copy(
            part, part, psend.at[q, src_chip], precv.at[q, src_chip],
            device_id={"col": partner}, device_id_type=MESH,
        )

    def far(way, q):
        return nz // 2 if way == q else nz // 2 - 1

    def relay(d, q):
        for way in range(2):
            if d:
                arrival(way, d, q).wait_recv()
            for r in [STRIDES[q]] + list(range(1, STRIDES[q])):
                if d + r <= far(way, q):
                    hop(way, d, q, r).start()
        for way in range(2 if d else 1):
            across(chip((2 * way - 1) * d), q).start()

    def settle(first, q):
        for way in range(2):
            for d in range(first, first + STRIDES[q]):
                if d % STRIDES[q] and d <= far(way, q) or d == nz // 2 == far(way, q):
                    arrival(way, d, q).wait_recv()
                    across(chip((2 * way - 1) * d), q).start()

    def steps_of(q):
        steps, relays = [], range(0, nz // 2, STRIDES[q])
        for d in relays:
            steps.append([functools.partial(relay, d, q)])
            if d:
                steps[-1].append(functools.partial(settle, d - STRIDES[q] + 1, q))
        steps.append([functools.partial(settle, relays[-1] + 1, q)])
        return steps

    early, late = steps_of(0), steps_of(1)

    def run(step):
        for part in step:
            part()

    def run_late(point):
        for _ in range(PLAN[point]):
            if late:
                run(late.pop(0))

    for i, step in enumerate(early):
        run(step)
        if i < len(early) - 1:
            run_late(i)

    def partner_done(q):
        def body(i, carry):
            from_partner(i, q).wait_recv()
            return carry
        lax.fori_loop(0, nz, body, 0)

    for copy in local:
        copy.wait()

    def window(rnd, sweep, w):
        vtile = (0, 2, 3, 5)[rnd]
        ttile = (1, 1, 4, 4)[rnd]
        row = sweep * NWIN + w
        vt = split(gath[pl.ds(8 * vtile + row, NREF, stride=SROWS), :])
        packed = gath[pl.ds(8 * ttile + row, NREF, stride=SROWS), :]
        tf = split(packed[:, NREF * (rnd % 2):NREF * (rnd % 2) + NREF])
        tv = split(dot3(tf, vt, ((1,), (0,))))
        return eye - dot3(vt, tv, ((0,), (0,)))

    def keep(his, los, at, value):
        his[at], los[at] = split(value)

    def build_outer(rnd):
        sent[rnd, 0] = window(rnd, 0, NWIN - 1)
        if_above(lambda: share(rnd, 0).start())
        sent[rnd, 1] = window(rnd, 0, 0)
        if_below(lambda: share(rnd, 1).start())

    def build(rnd):
        keep(first_hi, first_lo, NWIN, sent[rnd, 0])
        keep(first_hi, first_lo, 1, sent[rnd, 1])
        for w in range(1, NWIN - 1):
            keep(first_hi, first_lo, w + 1, window(rnd, 0, w))
        for w in range(NWIN):
            keep(second_hi, second_lo, w, window(rnd, 1, w))

    def offset(t):
        return off_ref[(t - 1) % 2, (t - 1) // 2] if t else 0

    lines = lax.broadcasted_iota(jnp.int32, (WR, NCOL), 0)
    end = jnp.where(p == nrow - 1, OWN, 2 * OWN)

    partner_done(0)
    build_outer(0)
    run_late(4)
    build(0)
    build_outer(1)
    for rnd in range(ROUNDS):
        old, new = rnd % 2, (rnd + 1) % 2
        before, a, b = offset(2 * rnd), offset(2 * rnd + 1), offset(2 * rnd + 2)
        extra = (b < a).astype(jnp.int32)
        low = a - WR * extra
        if rnd:
            build(rnd)
            if rnd == 2:
                build_outer(3)
        if_below(lambda: up(rnd).wait_recv())
        if_above(lambda: down(rnd).wait_recv())
        if_below(lambda: share(rnd, 0).wait_recv())
        if_above(lambda: share(rnd, 1).wait_recv())
        keep(first_hi, first_lo, 0, got[rnd, 0])
        keep(first_hi, first_lo, NWIN + 1, got[rnd, 1])

        @pl.when(p == 0)
        def _():
            mid[pl.ds(0, WR), :] = state[old][pl.ds(BELOW - WR + low - before, WR), :]

        for i in range(NWIN + 1):
            e = split(state[old][pl.ds(BELOW + WR * i + low - before, WR), :])
            k = i + 1 - extra
            value = dot3((first_hi[k], first_lo[k]), e, ((1,), (0,)))
            if i >= NWIN - 1:
                value = jnp.where(lines < end - low - WR * i, value, 0.0)
            mid[pl.ds(WR * (i + 1), WR), :] = value
        if rnd:
            if_below(lambda: down(rnd - 1).wait_send())
            if_above(lambda: up(rnd - 1).wait_send())
        for w in (3, 2, 0, 1):
            e = split(mid[pl.ds(WR * (w + 1) + b - low, WR), :])
            value = dot3((second_hi[w], second_lo[w]), e, ((1,), (0,)))
            if w == NWIN - 1:
                value = jnp.where(lines < end - b - WR * w, value, 0.0)
            state[new][pl.ds(BELOW + WR * w, WR), :] = value
            if rnd == ROUNDS - 1:
                last[pl.ds(WR * w, WR), :] = value
            if w == (3 if rnd == ROUNDS - 1 else 2):
                if_above(lambda: up(rnd + 1).start())
        if rnd < ROUNDS - 1:
            if_below(lambda: down(rnd + 1).start())

        @pl.when(p == 0)
        def _():
            state[new][pl.ds(BELOW - WR, WR), :] = mid[pl.ds(b - low, WR), :]

        if rnd < 2:
            run_late(5 + rnd)
        if rnd == 1:
            while late:
                run(late.pop(0))
            partner_done(1)
            build_outer(2)

    par = ROUNDS % 2
    result = mid
    shift = BELOW - offset(2 * ROUNDS)
    result[pl.ds(WR, 3 * WR), :] = last[pl.ds(WR - offset(2 * ROUNDS), 3 * WR), :]
    tail = pltpu.make_async_copy(
        result.at[pl.ds(WR, 3 * WR)], out_ref.at[pl.ds(WR, 3 * WR)], lsem.at[0]
    )
    tail.start()
    if_below(lambda: up(ROUNDS).wait_recv())
    result[pl.ds(0, WR), :] = state[par][pl.ds(shift, WR), :]
    head = pltpu.make_async_copy(result.at[pl.ds(0, WR)], out_ref.at[pl.ds(0, WR)], lsem.at[1])
    head.start()

    if_below(lambda: down(ROUNDS - 1).wait_send())
    if_above(lambda: up(ROUNDS - 1).wait_send())
    if_above(lambda: up(ROUNDS).wait_send())
    for rnd in range(ROUNDS):
        if_above(lambda: share(rnd, 0).wait_send())
        if_below(lambda: share(rnd, 1).wait_send())

    def drain(i, carry):
        for q in range(CHUNKS):
            across(i, q).wait_send()
        return carry

    lax.fori_loop(0, nz, drain, 0)
    for q in range(CHUNKS):
        for way in range(2):
            def drain_z(d, carry, way=way, q=q):
                arrival(way, d, q).wait_send()
                return carry
            lax.fori_loop(1, far(way, q) + 1, drain_z, 0)
    tail.wait()
    head.wait()


def shards(evecs, offsets, refl):
    nrow, ncol = lax.axis_size("row"), lax.axis_size("col")
    nz = ncol // 2
    vec = lambda rows: pltpu.VMEM((rows, NCOL), F32)
    sem = pltpu.SemaphoreType.DMA
    reach = nz // 2 + 1
    return pl.pallas_call(
        functools.partial(kernel, nrow, nz),
        out_shape=jax.ShapeDtypeStruct((NWIN * WR, NCOL), F32),
        in_specs=[
            pl.BlockSpec(memory_space=pl.ANY),
            pl.BlockSpec(memory_space=pltpu.VMEM),
            pl.BlockSpec(memory_space=pl.ANY),
        ],
        out_specs=pl.BlockSpec(memory_space=pl.ANY),
        scratch_shapes=[
            vec(ncol * SROWS),
            vec(BELOW + OWN + 2 * WR), vec(BELOW + OWN + 2 * WR), vec((NWIN + 2) * WR), vec(OWN),
            pltpu.VMEM((ROUNDS, 2, WR, WR), F32), pltpu.VMEM((ROUNDS, 2, WR, WR), F32),
            pltpu.VMEM((NWIN + 2, WR, WR), BF16), pltpu.VMEM((NWIN + 2, WR, WR), BF16),
            pltpu.VMEM((NWIN, WR, WR), BF16), pltpu.VMEM((NWIN, WR, WR), BF16),
            sem((2, CHUNKS, reach)), sem((2, CHUNKS, reach)),
            sem((CHUNKS, nz)), sem((CHUNKS, nz)),
            sem((2, 2)), sem((2, 2)), sem((ROUNDS, 2)), sem((ROUNDS, 2)), sem((2,)),
            pltpu.SMEM((2, ROUNDS), jnp.int32),
        ],
        compiler_params=pltpu.CompilerParams(collective_id=0, has_side_effects=True),
        name="sweeps",
    )(offsets.T, refl, evecs)


def solution(mesh):
    placed = (P("row", "col"), P(), P(None, None, "row", "col", None))
    return jax.shard_map(
        shards, mesh=mesh, in_specs=placed, out_specs=P("row", "col"), check_vma=False
    )
```
